256 devices in a mesh: row: 16 (over y_lo, x, core), col: 16 (over y_hi, z).
Axes of the slice: x: 4, y: 4 (y_hi: 2, y_lo: 2; y = y_hi * 2 + y_lo), z: 8, core: 2. Of those that a mesh axis runs over, the one named last changes fastest.
Arguments:
- amplitudes: bfloat16 [12288, 3072], P('row', 'col'), may hold values from -6 to 6
- integrals: bfloat16 [16, 192, 24576], P(None, 'row', 'col'), may hold values from -0.109375 to 0.109375
- residual_in: bfloat16 [12288, 24576], P('row', 'col'), may hold values from -3 to 3
- pair_class: int32 [128], P('row'), may hold values from 0 to 1
- cd_class: int32 [32], replicated, may hold values from 0 to 1
- ab_class: int32 [256], P('col'), may hold values from 0 to 1
Outputs:
- residual_out: bfloat16 [12288, 24576], P('row', 'col')
The draws below stay inside these ranges and needn't reach their ends.
All inputs are finite; a program needn't handle non-finite values.
Results may differ from the reference program's by a relative error of at most 0.001.
Values may be sent and summed in bfloat16 or wider, within the bound.
No kernel may reach another device: no remote copies, remote signals or barrier semaphores. Data moves between devices by JAX's collectives and lax.ppermute only.
A program may use at most 128 MiB of HBM per device.

```python
import jax
import jax.numpy as jnp
from jax import lax

TILE = 96
PDEV = 768
K = 3072
GROUPS = 16
KG = 192
P_SIZE = 12288
M = 24576
N_ROW = 16


def set_ends(values, own_key, low, top_value):
    spot = [jax.random.randint(jax.random.fold_in(own_key, axis), (), 0, length) for axis, length in enumerate(values.shape)]
    longest = values.shape.index(max(values.shape))
    beside = spot[:longest] + [(spot[longest] + 1) % values.shape[longest]] + spot[longest + 1:]
    return values.at[tuple(spot)].set(low).at[tuple(beside)].set(top_value)


def steps_of(stream_key, extent, split, smallest, largest):
    level = 1.0
    for axis_at, parts in split:
        steps = jax.random.uniform(jax.random.fold_in(jax.random.fold_in(stream_key, 6), axis_at), (parts,), jnp.float32, smallest / len(split), largest / len(split))
        level = level * jnp.repeat(jnp.exp(steps), extent[axis_at] // parts).reshape((-1,) + (1,) * (len(extent) - 1 - axis_at))
    return level


def noise(stream_key, dims, scale, most, shards=(), dtype=jnp.bfloat16):
    array = scale * jax.random.normal(stream_key, dims, jnp.float32)
    if shards:
        array = array * steps_of(stream_key, dims, shards, -0.22, 0.18)
    return jnp.clip(array, -most, most).astype(dtype)


def setup_inputs(seed: int = 0) -> dict:
    key_list = jax.random.split(jax.random.key(seed), 7)
    amplitudes = noise(key_list[0], (P_SIZE, K), 1.0, 6.0, ((0, 16), (1, 16)))
    integrals = noise(key_list[1], (GROUPS, KG, M), K ** -0.5, 0.109375, ((1, 16), (2, 16)))
    residual_in = noise(key_list[2], (P_SIZE, M), 0.5, 3.0, ((0, 16), (1, 16)))
    pair_class = set_ends(jax.random.randint(key_list[3], (P_SIZE // TILE,), 0, 2), jax.random.fold_in(key_list[3], 1), 0, 1).astype(jnp.int32)
    cd_class = set_ends(jax.random.randint(key_list[4], (K // TILE,), 0, 2), jax.random.fold_in(key_list[4], 1), 0, 1).astype(jnp.int32)
    ab_class = set_ends(jax.random.randint(key_list[5], (M // TILE,), 0, 2), jax.random.fold_in(key_list[5], 1), 0, 1).astype(jnp.int32)
    return dict(amplitudes=amplitudes, integrals=integrals, residual_in=residual_in, pair_class=pair_class, cd_class=cd_class, ab_class=ab_class)


def reference(amplitudes, integrals, residual_in, pair_class, cd_class, ab_class):
    pair_labels = jnp.repeat(pair_class, TILE)
    cd_labels = jnp.repeat(cd_class, TILE)
    ab_labels = jnp.repeat(ab_class, TILE)
    nothing = jnp.zeros((), jnp.bfloat16)
    masked_amp = jnp.where(pair_labels[:, None] == cd_labels[None, :], amplitudes, nothing)
    flat_int = integrals.reshape(K, M)
    masked_int = jnp.where(cd_labels[:, None] == ab_labels[None, :], flat_int, nothing)

    def row_block(pair_item):
        amp_rows, prior_rows = pair_item
        ladder = jnp.dot(amp_rows, masked_int, preferred_element_type=jnp.float32)
        return (prior_rows.astype(jnp.float32) + ladder).astype(jnp.bfloat16)

    result = lax.map(row_block, (masked_amp.reshape(N_ROW, PDEV, K), residual_in.reshape(N_ROW, PDEV, M)))
    return result.reshape(P_SIZE, M)
```

```python
import jax
import jax.numpy as jnp
import numpy as np
from jax import lax
from jax.sharding import Mesh, PartitionSpec as P

TILE = 96
FINE = ("ylo", "x", "core", "yhi", "z")
ROW = ("ylo", "x", "core")
COL = ("yhi", "z")


def shift(value, axis, steps):
    count = lax.axis_size(axis)
    return lax.ppermute(value, axis, [(i, (i + steps) % count) for i in range(count)])


def gather_amp(own):
    deep, wide = own.shape
    half = deep // 2
    count = lax.axis_size("z")
    z, side = lax.axis_index("z"), lax.axis_index("yhi")
    other = shift(own, "yhi", 1)
    found = []
    for chunk, plane in ((own, side), (other, 1 - side)):
        found.append((chunk, plane, z, 0))
        up = down = chunk
        for step in range(1, count // 2):
            up, down = shift(up, "z", 1), shift(down, "z", -1)
            found.append((up, plane, (z - step) % count, 0))
            found.append((down, plane, (z + step) % count, 0))
        far = (z + count // 2) % count
        found.append((shift(up[:half], "z", 1), plane, far, 0))
        found.append((shift(down[half:], "z", -1), plane, far, half))
    whole = jnp.zeros((2 * count, deep, wide), own.dtype)
    for chunk, plane, place, row in found:
        whole = lax.dynamic_update_slice(whole, chunk[None], (plane * count + place, row, 0))
    return whole


def local(amplitudes, integrals, residual_in, pair_class, cd_class, ab_class):
    groups, part, width = integrals.shape
    rows = 16
    deep = amplitudes.shape[1]
    pair_labels = jnp.repeat(pair_class, TILE)
    ab_labels = jnp.repeat(ab_class, TILE)
    group = lax.axis_index("yhi") * 8 + lax.axis_index("z")
    own_labels = lax.dynamic_slice_in_dim(jnp.repeat(cd_class, TILE), group * deep, deep)

    panel = lax.all_gather(integrals.reshape(groups * part, width), ROW, axis=0, tiled=True)

    own = jnp.where(own_labels[:, None] == pair_labels[None, :], amplitudes.T, 0)
    whole = gather_amp(own.astype(jnp.bfloat16))
    amp = whole.reshape(groups, rows, part, -1).transpose(1, 0, 2, 3).reshape(groups * deep, -1)

    ladder = lax.dot_general(amp, panel, (((0,), (0,)), ((), ())), preferred_element_type=jnp.float32)
    ladder = jnp.where(pair_labels[:, None] == ab_labels[None, :], ladder, 0.0)
    return (residual_in.astype(jnp.float32) + ladder).astype(jnp.bfloat16)


def solution(mesh):
    fine = Mesh(mesh.devices.reshape(2, 4, 2, 2, 8), FINE)
    return jax.shard_map(
        local,
        mesh=fine,
        in_specs=(P(ROW, COL), P(None, ROW, COL), P(ROW, COL), P(ROW), P(), P(COL)),
        out_specs=P(ROW, COL),
        check_vma=False,
    )
```

```python
import functools

import jax
import jax.numpy as jnp
from jax import lax
from jax.experimental import pallas as pl
from jax.experimental.pallas import tpu as pltpu
from jax.sharding import Mesh, PartitionSpec as P

TILE = 96
FINE = ("ylo", "x", "core", "yhi", "z")
ROW = ("ylo", "x", "core")
COL = ("yhi", "z")


def shift(value, axis, steps):
    count = lax.axis_size(axis)
    return lax.ppermute(value, axis, [(i, (i + steps) % count) for i in range(count)])


def after(values, earlier):
    return lax.optimization_barrier((tuple(values), tuple(earlier)))[0]


def ring(own):
    count = lax.axis_size("z")
    other = shift(own, "yhi", 1)
    found = [(own, 0, 0), (other, 1, 0)]
    ends = [(own, own), (other, other)]
    for step in range(1, count // 2):
        for plane in (0, 1):
            up, down = ends[plane]
            up, down = ends[plane] = (shift(up, "z", 1), shift(down, "z", -1))
            found += [(up, plane, -step), (down, plane, step)]
    for plane, way in ((0, 1), (1, -1)):
        (last,) = after(ends[plane][plane : plane + 1], ends[plane])
        found.append((shift(last, "z", way), plane, count // 2))
    return found


def mask_kernel(pair_ref, cd_ref, amp_ref, out_ref):
    group = lax.axis_index("yhi") * lax.axis_size("z") + lax.axis_index("z")
    column = lax.broadcasted_iota(jnp.int32, (1, amp_ref.shape[1]), 1)
    labels = jnp.full(column.shape, pair_ref[0])
    for tile in range(1, pair_ref.shape[0]):
        labels = jnp.where(column >= tile * TILE, pair_ref[tile], labels)
    for tile in range(amp_ref.shape[0] // TILE):
        rows = slice(tile * TILE, (tile + 1) * TILE)
        kept = labels == cd_ref[group * 2 + tile]
        out_ref[rows] = jnp.where(kept, amp_ref[rows].astype(jnp.float32), 0.0).astype(out_ref.dtype)


def masked(amplitudes, pair_class, cd_class):
    smem = pl.BlockSpec(memory_space=pltpu.SMEM)
    vmem = pl.BlockSpec(memory_space=pltpu.VMEM)
    return pl.pallas_call(
        mask_kernel,
        out_shape=jax.ShapeDtypeStruct(amplitudes.shape, amplitudes.dtype),
        in_specs=[smem, smem, vmem],
        out_specs=vmem,
        compiler_params=pltpu.CompilerParams(vmem_limit_bytes=24 << 20),
        name="mask_amplitudes",
    )(pair_class, cd_class, amplitudes)


def ordered(integrals, order):
    groups, part, width = integrals.shape
    flat = integrals.transpose(1, 0, 2).reshape(part * groups, width)
    place = jnp.arange(part, dtype=jnp.int32)[None, :] * groups + order[:, None]
    chosen = place.reshape(-1, 1) == jnp.arange(part * groups, dtype=jnp.int32)[None, :]
    return jnp.dot(chosen.astype(integrals.dtype), flat, preferred_element_type=jnp.float32).astype(integrals.dtype)


def arrange(chunk_refs, out_ref):
    wide, part = 128, 12

    @pl.loop(0, out_ref.shape[0] // wide)
    def _(step):
        lanes = pl.ds(pl.multiple_of(step * wide, wide), wide)
        size = out_ref.shape[1] // 4
        for quad in range(4):
            pieces = [[], [], [], []]
            for pair in (0, 2):
                at = (quad * 4 + pair) * part
                for chunk in chunk_refs:
                    both = chunk[at : at + 2 * part, lanes].astype(jnp.float32)
                    pieces[pair].append(both[:part])
                    pieces[pair + 1].append(both[part:])
            block = jnp.concatenate(sum(pieces, []))
            out_ref[lanes, quad * size : (quad + 1) * size] = block.T.astype(out_ref.dtype)


def arranged(chunks):
    deep, wide = chunks[0].shape
    return pl.pallas_call(
        lambda *refs: arrange(refs[:-1], refs[-1]),
        out_shape=jax.ShapeDtypeStruct((wide, len(chunks) * deep), chunks[0].dtype),
        in_specs=[pl.BlockSpec(memory_space=pltpu.VMEM)] * len(chunks),
        out_specs=pl.BlockSpec(memory_space=pltpu.VMEM),
        compiler_params=pltpu.CompilerParams(vmem_limit_bytes=24 << 20),
        cost_estimate=pl.CostEstimate(flops=10**8, bytes_accessed=10**7, transcendentals=0),
        name="arrange_amplitudes",
    )(*chunks)


def product_kernel(block, pair_ref, ab_ref, early_ref, late_ref, panel_ref, prior_ref, out_ref, late, held, prior, done, late_sem, sems):
    in_sem, prior_sem, out_sem = (sems.at[i] for i in range(3))
    deep, half = early_ref.shape[1], panel_ref.shape[1] // 2
    steps = out_ref.shape[1] // block

    def columns(step):
        return pl.ds(pl.multiple_of(step * block, block), block)

    def fetch(step):
        return pltpu.make_async_copy(panel_ref.at[:, :, columns(step)], held.at[:, :, columns(step)], in_sem.at[step])

    def put(step):
        return pltpu.make_async_copy(done.at[:, columns(step)], out_ref.at[:, columns(step)], out_sem.at[step])

    def fetch_prior(step):
        return pltpu.make_async_copy(prior_ref.at[:, columns(step)], prior.at[:, columns(step)], prior_sem.at[step])

    fetch_late = pltpu.make_async_copy(late_ref, late, late_sem)
    fetch_late.start()
    for step in range(steps):
        fetch(step).start()
        fetch_prior(step).start()
    fetch_late.wait()

    @pl.loop(0, steps)
    def _(step):
        fetch(step).wait()
        lanes = columns(step)
        column = step * block + lax.broadcasted_iota(jnp.int32, (1, block), 1)
        labels = jnp.full((1, block), ab_ref[0])
        for tile in range(1, ab_ref.shape[0]):
            labels = jnp.where(column >= tile * TILE, ab_ref[tile], labels)
        ladder = sum(
            jnp.dot(amp[...], held[:, at : at + half, lanes].reshape(deep, block), preferred_element_type=jnp.float32)
            for amp, at in ((early_ref, 0), (late, half))
        )
        fetch_prior(step).wait()
        for tile in range(out_ref.shape[0] // TILE):
            rows = slice(tile * TILE, (tile + 1) * TILE)
            kept = jnp.where(labels == pair_ref[tile], ladder[rows], 0.0)
            done[rows, lanes] = (prior[rows, lanes].astype(jnp.float32) + kept).astype(done.dtype)
        put(step).start()

    for step in range(steps):
        put(step).wait()


def finished(early, late, panel, prior, pair_class, ab_class):
    high, deep = early.shape
    width = panel.shape[2]
    block = 256
    steps = width // block
    smem, vmem = (pl.BlockSpec(memory_space=space) for space in (pltpu.SMEM, pltpu.VMEM))
    hbm = pl.BlockSpec(memory_space=pltpu.HBM)
    keep = pltpu.with_memory_space_constraint
    return pl.pallas_call(
        functools.partial(product_kernel, block),
        out_shape=jax.ShapeDtypeStruct(prior.shape, prior.dtype),
        in_specs=[smem, smem, vmem, hbm, hbm, hbm],
        out_specs=hbm,
        scratch_shapes=[
            pltpu.VMEM(late.shape, late.dtype),
            pltpu.VMEM(panel.shape, panel.dtype),
            pltpu.VMEM(prior.shape, prior.dtype),
            pltpu.VMEM(prior.shape, prior.dtype),
            pltpu.SemaphoreType.DMA,
            pltpu.SemaphoreType.DMA((3, steps)),
        ],
        compiler_params=pltpu.CompilerParams(vmem_limit_bytes=24 << 20),
        cost_estimate=pl.CostEstimate(flops=4 * high * deep * width, bytes_accessed=4 * deep * width, transcendentals=0),
        name="product",
    )(pair_class, ab_class, keep(early, pltpu.VMEM), keep(late, pltpu.HBM), keep(panel, pltpu.HBM), keep(prior, pltpu.HBM))


def local(amplitudes, integrals, residual_in, pair_class, cd_class, ab_class):
    count = lax.axis_size("z")
    z, side = lax.axis_index("z"), lax.axis_index("yhi")
    found = ring(masked(amplitudes.T, pair_class, cd_class))
    order = jnp.stack([(side ^ plane) * count + (z + step) % count for _, plane, step in found])
    panel = lax.all_gather(ordered(integrals, order), ROW, axis=0)
    half = len(found) // 2
    chunks = [chunk for chunk, _, _ in found]
    return finished(arranged(chunks[:half]), arranged(chunks[half:]), panel, residual_in, pair_class, ab_class)


def solution(mesh):
    fine = Mesh(mesh.devices.reshape(2, 4, 2, 2, 8), FINE)
    return jax.shard_map(
        local,
        mesh=fine,
        in_specs=(P(ROW, COL), P(None, ROW, COL), P(ROW, COL), P(ROW), P(), P(COL)),
        out_specs=P(ROW, COL),
        check_vma=False,
    )
```

```python
import functools

import jax
import jax.numpy as jnp
from jax import lax
from jax.experimental import pallas as pl
from jax.experimental.pallas import tpu as pltpu
from jax.sharding import Mesh, PartitionSpec as P

TILE = 96
FINE = ("ylo", "x", "core", "yhi", "z")
ROW = ("ylo", "x", "core")
COL = ("yhi", "z")


def shift(value, axis, steps):
    count = lax.axis_size(axis)
    return lax.ppermute(value, axis, [(i, (i + steps) % count) for i in range(count)])


def after(values, earlier):
    return lax.optimization_barrier((tuple(values), tuple(earlier)))[0]


def ring(own):
    count = lax.axis_size("z")
    other = shift(own, "yhi", 1)
    found = [(own, 0, 0), (other, 1, 0)]
    ends = [(own, own), (other, other)]
    for step in range(1, count // 2):
        for plane in (0, 1):
            up, down = ends[plane]
            up, down = ends[plane] = (shift(up, "z", 1), shift(down, "z", -1))
            found += [(up, plane, -step), (down, plane, step)]
    for plane, way in ((0, 1), (1, -1)):
        (last,) = after(ends[plane][plane : plane + 1], ends[plane])
        found.append((shift(last, "z", way), plane, count // 2))
    return found


def ordered(integrals, order):
    groups, part, width = integrals.shape
    flat = integrals.transpose(1, 0, 2).reshape(part * groups, width)
    place = jnp.arange(part, dtype=jnp.int32)[None, :] * groups + order[:, None]
    chosen = place.reshape(-1, 1) == jnp.arange(part * groups, dtype=jnp.int32)[None, :]
    return jnp.dot(chosen.astype(integrals.dtype), flat, preferred_element_type=jnp.float32).astype(integrals.dtype)


def group_of(plane, step):
    count = lax.axis_size("z")
    return lax.rem(lax.axis_index("yhi") + plane, 2) * count + lax.rem(lax.axis_index("z") + step + count, count)


def arrange_kernel(places, pair_ref, cd_ref, *refs):
    *chunk_refs, out_ref = refs
    wide, part = 128, 12
    size = out_ref.shape[1] // 4
    steps = out_ref.shape[0] // wide
    classes = [[cd_ref[2 * group_of(*place) + tile] for tile in (0, 1)] for place in places]

    @pl.loop(0, steps)
    def _(step):
        lanes = pl.ds(pl.multiple_of(step * wide, wide), wide)
        column = step * wide + lax.broadcasted_iota(jnp.int32, (1, wide), 1)
        labels = jnp.full(column.shape, pair_ref[0])
        for tile in range(1, pair_ref.shape[0]):
            labels = jnp.where(column >= tile * TILE, pair_ref[tile], labels)
        for quad in range(4):
            keep = [labels == both[quad // 2] for both in classes]
            pieces = [[], [], [], []]
            for pair in (0, 2):
                at = (quad * 4 + pair) * part
                for chunk, kept in zip(chunk_refs, keep):
                    both = jnp.where(kept, chunk[at : at + 2 * part, lanes].astype(jnp.float32), 0.0)
                    pieces[pair].append(both[:part])
                    pieces[pair + 1].append(both[part:])
            block = jnp.concatenate(sum(pieces, []))
            out_ref[lanes, quad * size : (quad + 1) * size] = block.T.astype(out_ref.dtype)


def arranged(found, pair_class, cd_class):
    chunks = [chunk for chunk, _, _ in found]
    deep, wide = chunks[0].shape
    shape = (wide, len(chunks) * deep)
    smem, vmem = (pl.BlockSpec(memory_space=space) for space in (pltpu.SMEM, pltpu.VMEM))
    return pl.pallas_call(
        functools.partial(arrange_kernel, [place for _, *place in found]),
        out_shape=jax.ShapeDtypeStruct(shape, chunks[0].dtype),
        in_specs=[smem, smem] + [vmem] * len(chunks),
        out_specs=vmem,
        compiler_params=pltpu.CompilerParams(vmem_limit_bytes=24 << 20),
        cost_estimate=pl.CostEstimate(flops=10**8, bytes_accessed=10**7, transcendentals=0),
        name="arrange_amplitudes",
    )(pair_class, cd_class, *chunks)


def product_kernel(block, pair_ref, ab_ref, early_ref, late_ref, panel_ref, prior_ref, out_ref, late, held, prior, done, late_sem, sems):
    in_sem, prior_sem, out_sem = (sems.at[i] for i in range(3))
    deep, half = early_ref.shape[1], panel_ref.shape[1] // 2
    steps = out_ref.shape[1] // block

    def columns(step):
        return pl.ds(pl.multiple_of(step * block, block), block)

    def fetch(step):
        return pltpu.make_async_copy(panel_ref.at[:, :, columns(step)], held.at[:, :, columns(step)], in_sem.at[step])

    def put(step):
        return pltpu.make_async_copy(done.at[:, columns(step)], out_ref.at[:, columns(step)], out_sem.at[step])

    def fetch_prior(step):
        return pltpu.make_async_copy(prior_ref.at[:, columns(step)], prior.at[:, columns(step)], prior_sem.at[step])

    def times(amp, at, lanes):
        panel = held[:, at : at + half, lanes].reshape(deep, block)
        return jnp.dot(amp[...], panel, preferred_element_type=jnp.float32)

    def finish(step, ladder):
        lanes = columns(step)
        column = step * block + lax.broadcasted_iota(jnp.int32, (1, block), 1)
        labels = jnp.full((1, block), ab_ref[0])
        for tile in range(1, ab_ref.shape[0]):
            labels = jnp.where(column >= tile * TILE, ab_ref[tile], labels)
        fetch_prior(step).wait()
        for tile in range(out_ref.shape[0] // TILE):
            rows = slice(tile * TILE, (tile + 1) * TILE)
            kept = jnp.where(labels == pair_ref[tile], ladder[rows], 0.0)
            done[rows, lanes] = (prior[rows, lanes].astype(jnp.float32) + kept).astype(done.dtype)
        put(step).start()

    fetch_late = pltpu.make_async_copy(late_ref, late, late_sem)
    fetch(0).start()
    fetch_late.start()
    fetch_prior(0).start()
    fetch(0).wait()
    fetch_late.wait()
    for step in range(1, steps):
        fetch(step).start()
        fetch_prior(step).start()
    finish(0, times(early_ref, 0, pl.ds(0, block)) + times(late, half, pl.ds(0, block)))

    @pl.loop(1, steps)
    def _(step):
        fetch(step).wait()
        finish(step, times(early_ref, 0, columns(step)) + times(late, half, columns(step)))

    for step in range(steps):
        put(step).wait()


def finished(early, late, panel, prior, pair_class, ab_class):
    high, deep = early.shape
    width = panel.shape[2]
    block = 256
    steps = width // block
    smem, vmem = (pl.BlockSpec(memory_space=space) for space in (pltpu.SMEM, pltpu.VMEM))
    hbm = pl.BlockSpec(memory_space=pltpu.HBM)
    keep = pltpu.with_memory_space_constraint
    return pl.pallas_call(
        functools.partial(product_kernel, block),
        out_shape=jax.ShapeDtypeStruct(prior.shape, prior.dtype),
        in_specs=[smem, smem, vmem, hbm, hbm, hbm],
        out_specs=hbm,
        scratch_shapes=[
            pltpu.VMEM(late.shape, late.dtype),
            pltpu.VMEM(panel.shape, panel.dtype),
            pltpu.VMEM(prior.shape, prior.dtype),
            pltpu.VMEM(prior.shape, prior.dtype),
            pltpu.SemaphoreType.DMA,
            pltpu.SemaphoreType.DMA((3, steps)),
        ],
        compiler_params=pltpu.CompilerParams(vmem_limit_bytes=24 << 20),
        cost_estimate=pl.CostEstimate(flops=4 * high * deep * width, bytes_accessed=4 * deep * width, transcendentals=0),
        name="product",
    )(pair_class, ab_class, keep(early, pltpu.VMEM), keep(late, pltpu.HBM), keep(panel, pltpu.HBM), keep(prior, pltpu.HBM))


def local(amplitudes, integrals, residual_in, pair_class, cd_class, ab_class):
    found = ring(amplitudes.T)
    order = jnp.stack([group_of(*place) for _, *place in found])
    panel = lax.all_gather(ordered(integrals, order), ROW, axis=0)
    half = len(found) // 2
    early = arranged(found[:half], pair_class, cd_class)
    late = arranged(found[half:], pair_class, cd_class)
    return finished(early, late, panel, residual_in, pair_class, ab_class)


def solution(mesh):
    fine = Mesh(mesh.devices.reshape(2, 4, 2, 2, 8), FINE)
    return jax.shard_map(
        local,
        mesh=fine,
        in_specs=(P(ROW, COL), P(None, ROW, COL), P(ROW, COL), P(ROW), P(), P(COL)),
        out_specs=P(ROW, COL),
        check_vma=False,
    )
```

```python
import functools

import jax
import jax.numpy as jnp
from jax import lax
from jax.experimental import pallas as pl
from jax.experimental.pallas import tpu as pltpu
from jax.sharding import Mesh, PartitionSpec as P

TILE = 96
FINE = ("ylo", "x", "core", "yhi", "z")
ROW = ("ylo", "x", "core")
COL = ("yhi", "z")


def shift(value, axis, steps):
    count = lax.axis_size(axis)
    return lax.ppermute(value, axis, [(i, (i + steps) % count) for i in range(count)])


def after(values, earlier):
    return lax.optimization_barrier((tuple(values), tuple(earlier)))[0]


def ring(own):
    count = lax.axis_size("z")
    other = shift(own, "yhi", 1)
    found = [(own, 0, 0), (other, 1, 0)]
    ends = [(own, own), (other, other)]
    for step in range(1, count // 2):
        for plane in (0, 1):
            up, down = ends[plane]
            up, down = ends[plane] = (shift(up, "z", 1), shift(down, "z", -1))
            found += [(up, plane, -step), (down, plane, step)]
    for plane, way in ((0, 1), (1, -1)):
        (last,) = after(ends[plane][plane : plane + 1], ends[plane])
        found.append((shift(last, "z", way), plane, count // 2))
    return found


def ordered(integrals, order):
    groups, part, width = integrals.shape
    flat = integrals.transpose(1, 0, 2).reshape(part * groups, width)
    place = jnp.arange(part, dtype=jnp.int32)[None, :] * groups + order[:, None]
    chosen = place.reshape(-1, 1) == jnp.arange(part * groups, dtype=jnp.int32)[None, :]
    return jnp.dot(chosen.astype(integrals.dtype), flat, preferred_element_type=jnp.float32).astype(integrals.dtype)


def group_of(plane, step):
    count = lax.axis_size("z")
    return lax.rem(lax.axis_index("yhi") + plane, 2) * count + lax.rem(lax.axis_index("z") + step + count, count)


def arrange_kernel(places, pair_ref, cd_ref, *refs):
    *chunk_refs, out_ref = refs
    wide, part = 128, 12
    size = out_ref.shape[1] // 4
    steps = out_ref.shape[0] // wide
    classes = [[cd_ref[2 * group_of(*place) + tile] for tile in (0, 1)] for place in places]

    @pl.loop(0, steps)
    def _(step):
        lanes = pl.ds(pl.multiple_of(step * wide, wide), wide)
        column = step * wide + lax.broadcasted_iota(jnp.int32, (1, wide), 1)
        labels = jnp.full(column.shape, pair_ref[0])
        for tile in range(1, pair_ref.shape[0]):
            labels = jnp.where(column >= tile * TILE, pair_ref[tile], labels)
        for quad in range(4):
            keep = [labels == both[quad // 2] for both in classes]
            pieces = [[], [], [], []]
            for pair in (0, 2):
                at = (quad * 4 + pair) * part
                for chunk, kept in zip(chunk_refs, keep):
                    both = jnp.where(kept, chunk[at : at + 2 * part, lanes].astype(jnp.float32), 0.0)
                    pieces[pair].append(both[:part])
                    pieces[pair + 1].append(both[part:])
            block = jnp.concatenate(sum(pieces, []))
            out_ref[lanes, quad * size : (quad + 1) * size] = block.T.astype(out_ref.dtype)


def arranged(found, pair_class, cd_class):
    chunks = [chunk for chunk, _, _ in found]
    deep, wide = chunks[0].shape
    shape = (wide, len(chunks) * deep)
    smem, vmem = (pl.BlockSpec(memory_space=space) for space in (pltpu.SMEM, pltpu.VMEM))
    return pl.pallas_call(
        functools.partial(arrange_kernel, [place for _, *place in found]),
        out_shape=jax.ShapeDtypeStruct(shape, chunks[0].dtype),
        in_specs=[smem, smem] + [vmem] * len(chunks),
        out_specs=vmem,
        compiler_params=pltpu.CompilerParams(vmem_limit_bytes=28 << 20),
        cost_estimate=pl.CostEstimate(flops=10**8, bytes_accessed=10**7, transcendentals=0),
        name="arrange_amplitudes",
    )(pair_class, cd_class, *chunks)


def product_kernel(block, pair_ref, ab_ref, early_ref, late_ref, panel_ref, prior_ref, out_ref, late, held, prior, done, late_sem, sems):
    in_sem, prior_sem, out_sem = (sems.at[i] for i in range(3))
    deep, half = early_ref.shape[1], panel_ref.shape[1] // 2
    steps = out_ref.shape[1] // block

    def columns(step):
        return pl.ds(pl.multiple_of(step * block, block), block)

    def fetch(step):
        return pltpu.make_async_copy(panel_ref.at[:, :, columns(step)], held.at[:, :, columns(step)], in_sem.at[step])

    def put(step):
        return pltpu.make_async_copy(done.at[:, columns(step)], out_ref.at[:, columns(step)], out_sem.at[step])

    def fetch_prior(step):
        return pltpu.make_async_copy(prior_ref.at[:, columns(step)], prior.at[:, columns(step)], prior_sem.at[step])

    def times(amp, at, lanes):
        panel = held[:, at : at + half, lanes].reshape(deep, block)
        return jnp.dot(amp[...], panel, preferred_element_type=jnp.float32)

    def finish(step, ladder):
        lanes = columns(step)
        column = step * block + lax.broadcasted_iota(jnp.int32, (1, block), 1)
        labels = jnp.full((1, block), ab_ref[0])
        for tile in range(1, ab_ref.shape[0]):
            labels = jnp.where(column >= tile * TILE, ab_ref[tile], labels)
        fetch_prior(step).wait()
        for tile in range(out_ref.shape[0] // TILE):
            rows = slice(tile * TILE, (tile + 1) * TILE)
            kept = jnp.where(labels == pair_ref[tile], ladder[rows], 0.0)
            done[rows, lanes] = (prior[rows, lanes].astype(jnp.float32) + kept).astype(done.dtype)
        put(step).start()

    fetch_late = pltpu.make_async_copy(late_ref, late, late_sem)
    fetch(0).start()
    fetch_late.start()
    fetch_prior(0).start()
    fetch(0).wait()
    fetch_late.wait()
    for step in range(1, steps):
        fetch(step).start()
        fetch_prior(step).start()
    finish(0, times(early_ref, 0, pl.ds(0, block)) + times(late, half, pl.ds(0, block)))

    @pl.loop(1, steps)
    def _(step):
        fetch(step).wait()
        finish(step, times(early_ref, 0, columns(step)) + times(late, half, columns(step)))

    for step in range(steps):
        put(step).wait()


def finished(early, late, panel, prior, pair_class, ab_class):
    high, deep = early.shape
    width = panel.shape[2]
    block = 512
    steps = width // block
    smem, vmem = (pl.BlockSpec(memory_space=space) for space in (pltpu.SMEM, pltpu.VMEM))
    hbm = pl.BlockSpec(memory_space=pltpu.HBM)
    keep = pltpu.with_memory_space_constraint
    return pl.pallas_call(
        functools.partial(product_kernel, block),
        out_shape=jax.ShapeDtypeStruct(prior.shape, prior.dtype),
        in_specs=[smem, smem, vmem, hbm, hbm, hbm],
        out_specs=hbm,
        scratch_shapes=[
            pltpu.VMEM(late.shape, late.dtype),
            pltpu.VMEM(panel.shape, panel.dtype),
            pltpu.VMEM(prior.shape, prior.dtype),
            pltpu.VMEM(prior.shape, prior.dtype),
            pltpu.SemaphoreType.DMA,
            pltpu.SemaphoreType.DMA((3, steps)),
        ],
        compiler_params=pltpu.CompilerParams(vmem_limit_bytes=28 << 20),
        cost_estimate=pl.CostEstimate(flops=4 * high * deep * width, bytes_accessed=4 * deep * width, transcendentals=0),
        name="product",
    )(pair_class, ab_class, keep(early, pltpu.VMEM), keep(late, pltpu.HBM), keep(panel, pltpu.HBM), keep(prior, pltpu.HBM))


def local(amplitudes, integrals, residual_in, pair_class, cd_class, ab_class):
    found = ring(amplitudes.T)
    order = jnp.stack([group_of(*place) for _, *place in found])
    panel = lax.all_gather(ordered(integrals, order), ROW, axis=0)
    half = len(found) // 2
    early = arranged(found[:half], pair_class, cd_class)
    late = arranged(found[half:], pair_class, cd_class)
    return finished(early, late, panel, residual_in, pair_class, ab_class)


def solution(mesh):
    fine = Mesh(mesh.devices.reshape(2, 4, 2, 2, 8), FINE)
    return jax.shard_map(
        local,
        mesh=fine,
        in_specs=(P(ROW, COL), P(None, ROW, COL), P(ROW, COL), P(ROW), P(), P(COL)),
        out_specs=P(ROW, COL),
        check_vma=False,
    )
```
